32 devices in a mesh: dp: 8 (over y, x, core), seq: 4 (over z).
Axes of the slice: x: 2, y: 2, z: 4, core: 2. Of those that a mesh axis runs over, the one named last changes fastest.
Arguments:
- image_tokens: bfloat16 [8, 1024, 1536], P('dp', 'seq'), may hold values from -6 to 6
- text_tokens: bfloat16 [8, 160, 1536], P('dp', 'seq'), may hold values from -6 to 6
- conditioning: bfloat16 [8, 1536], P('dp'), may hold values from -6 to 6
- live_text: int32 [8], P('dp'), may hold values from 1 to 160, as said below
- w_mod_img: bfloat16 [1536, 9216], P(None, ('dp', 'seq')), may hold values from -0.15625 to 0.15625
- w_mod_txt: bfloat16 [1536, 9216], P(None, ('dp', 'seq')), may hold values from -0.15625 to 0.15625
- w_qkv_img: bfloat16 [1536, 4608], P(('dp', 'seq')), may hold values from -0.15625 to 0.15625
- w_qkv_txt: bfloat16 [1536, 4608], P(('dp', 'seq')), may hold values from -0.15625 to 0.15625
- w_out_img: bfloat16 [1536, 1536], P(('dp', 'seq')), may hold values from -1.25 to 1.25
- w_out_txt: bfloat16 [1536, 1536], P(('dp', 'seq')), may hold values from -1.25 to 1.25
- w_up_img: bfloat16 [1536, 6144], P(('dp', 'seq')), may hold values from -0.15625 to 0.15625
- w_up_txt: bfloat16 [1536, 6144], P(('dp', 'seq')), may hold values from -0.15625 to 0.15625
- w_down_img: bfloat16 [6144, 1536], P(('dp', 'seq')), may hold values from -0.078125 to 0.078125
- w_down_txt: bfloat16 [6144, 1536], P(('dp', 'seq')), may hold values from -0.078125 to 0.078125
- image_cotangent: bfloat16 [8, 1024, 1536], P('dp', 'seq'), may hold values from -6 to 6
- text_cotangent: bfloat16 [8, 160, 1536], P('dp', 'seq'), may hold values from -6 to 6
Outputs:
- out_image: bfloat16 [8, 1024, 1536], P('dp', 'seq')
- out_text: bfloat16 [8, 160, 1536], P('dp', 'seq')
- grad_image: float32 [8, 1024, 1536], P('dp', 'seq')
- grad_text: float32 [8, 160, 1536], P('dp', 'seq')
- grad_cond: float32 [8, 1536], P('dp')
- grad_mod_img: float32 [1536, 9216], P(None, ('dp', 'seq'))
- grad_mod_txt: float32 [1536, 9216], P(None, ('dp', 'seq'))
- grad_qkv_img: float32 [1536, 4608], P(('dp', 'seq'))
- grad_qkv_txt: float32 [1536, 4608], P(('dp', 'seq'))
- grad_out_img: float32 [1536, 1536], P(('dp', 'seq'))
- grad_out_txt: float32 [1536, 1536], P(('dp', 'seq'))
- grad_up_img: float32 [1536, 6144], P(('dp', 'seq'))
- grad_up_txt: float32 [1536, 6144], P(('dp', 'seq'))
- grad_down_img: float32 [6144, 1536], P(('dp', 'seq'))
- grad_down_txt: float32 [6144, 1536], P(('dp', 'seq'))
The draws below stay inside these ranges and needn't reach their ends.
Inputs may be any that keep to these rules, and one draw needn't show every extreme that they name: Text tokens of index live_text[b] or more in sequence b are padding; some sequence has all 160 live.
All inputs are finite; a program needn't handle non-finite values.
Results may differ from the reference program's by a relative error of at most 0.015.
The reference program's roundings to bfloat16 on the way count: a program that leaves them out, or rounds other values in their place, can miss the bound.
Values may be sent and summed in bfloat16 or wider, within the bound.
No kernel may reach another device: no remote copies, remote signals or barrier semaphores. Data moves between devices by JAX's collectives and lax.ppermute only.
A program may use at most 384 MiB of HBM per device.

```python
import functools
import jax
import jax.numpy as jnp
from jax import lax

D = 1536
HEADS = 24
HEAD_DIM = 64
FF = 6144
IMG = 1024
TXT = 160
SEQS = 8


def draw_live_text(key, part):
    first_key, second_key = jax.random.split(key)
    counts = jax.random.randint(first_key, (SEQS,), 1, TXT + 1)
    target = jax.random.randint(second_key, (), 0, SEQS)
    return counts.at[target].set(TXT).astype(jnp.int32)


def block_scale(key, dims, cuts, low, largest):
    def one(position, shards_of):
        heights = jax.random.uniform(jax.random.fold_in(jax.random.fold_in(key, 6), position), (shards_of,), jnp.float32, low / len(cuts), largest / len(cuts))
        return jnp.repeat(jnp.exp(heights), dims[position] // shards_of).reshape((-1,) + (1,) * (len(dims) - position - 1))

    factor_of = one(*cuts[0])
    for cut in cuts[1:]:
        factor_of = factor_of * one(*cut)
    return factor_of


def scatter_about(own_key, extent, deviation, bound, cuts=(), held_as=jnp.bfloat16):
    array = jax.random.normal(own_key, extent, jnp.float32) * deviation
    if len(cuts) > 0:
        array = block_scale(own_key, extent, cuts, -0.22, 0.18) * array
    return jnp.clip(array, min=-bound, max=bound).astype(held_as)


def setup_inputs(seed: int = 0) -> dict:
    key_list = jax.random.split(jax.random.key(seed), 17)
    return {
        "image_tokens": scatter_about(key_list[0], (SEQS, IMG, D), 1.0, 6.0, ((0, 8), (1, 4))),
        "text_tokens": scatter_about(key_list[1], (SEQS, TXT, D), 1.0, 6.0, ((0, 8), (1, 4))),
        "conditioning": scatter_about(key_list[2], (SEQS, D), 1.0, 6.0, ((0, 8),)),
        "live_text": draw_live_text(jax.random.fold_in(key_list[16], 71), 0),
        "w_mod_img": scatter_about(key_list[4], (D, 6 * D), D ** -0.5, 0.15625, ((1, 32),)),
        "w_mod_txt": scatter_about(key_list[5], (D, 6 * D), D ** -0.5, 0.15625, ((1, 32),)),
        "w_qkv_img": scatter_about(key_list[6], (D, 3 * D), D ** -0.5, 0.15625, ((0, 32),)),
        "w_qkv_txt": scatter_about(key_list[7], (D, 3 * D), D ** -0.5, 0.15625, ((0, 32),)),
        "w_out_img": scatter_about(key_list[8], (D, D), (max(D // 64, 1)) ** -0.5, 1.25, ((0, 32),)),
        "w_out_txt": scatter_about(key_list[9], (D, D), (max(D // 64, 1)) ** -0.5, 1.25, ((0, 32),)),
        "w_up_img": scatter_about(key_list[10], (D, FF), D ** -0.5, 0.15625, ((0, 32),)),
        "w_up_txt": scatter_about(key_list[11], (D, FF), D ** -0.5, 0.15625, ((0, 32),)),
        "w_down_img": scatter_about(key_list[12], (FF, D), FF ** -0.5, 0.078125, ((0, 32),)),
        "w_down_txt": scatter_about(key_list[13], (FF, D), FF ** -0.5, 0.078125, ((0, 32),)),
        "image_cotangent": scatter_about(key_list[14], (SEQS, IMG, D), 1.0, 6.0, ((0, 8), (1, 4))),
        "text_cotangent": scatter_about(key_list[15], (SEQS, TXT, D), 1.0, 6.0, ((0, 8), (1, 4))),
    }


@jax.custom_vjp
def low(v):
    return lax.optimization_barrier(v.astype(jnp.bfloat16)).astype(jnp.float32)

@jax.custom_vjp
def low_back(v):
    return v

def low_keep(v):
    return (low(v), None)

def low_pass(kept, grad):
    return (grad,)

def back_keep(v):
    return (v, None)

def back_low(kept, grad):
    return (low(grad),)
low.defvjp(low_keep, low_pass)
low_back.defvjp(back_keep, back_low)
highest = lax.Precision.HIGHEST

def matmul(left, right):
    return jnp.dot(left, right, precision=highest)

def layer_norm(values):
    centre = values - lax.optimization_barrier(jnp.mean(values, axis=-1, keepdims=True))
    spread = lax.optimization_barrier(jnp.mean(centre * centre, axis=-1, keepdims=True))
    return centre * lax.rsqrt(spread + 1e-06)

def attend_head(queries, keys, values, key_live):
    raw = low_back(matmul(queries, keys.T))
    scores = jnp.where(key_live[None, :], raw * HEAD_DIM ** (-0.5), -1e+30)
    probs = jax.nn.softmax(scores, axis=-1)
    return low(low_back(matmul(low(probs), values)))

def project_in(tokens, mods, weight):
    normed = layer_norm(tokens)
    mixed = low(normed * (1.0 + mods[1]) + mods[0])
    return low(low_back(matmul(mixed, weight)))

def project_out(tokens, attended, mods, w_out, w_up, w_down):
    branch = low_back(matmul(attended, w_out))
    middle = tokens + mods[2] * branch
    mixed = low(layer_norm(middle) * (1.0 + mods[4]) + mods[3])
    hidden = low_back(matmul(mixed, w_up))
    activated = low(jax.nn.gelu(hidden, approximate=True))
    result = low_back(matmul(activated, w_down))
    return middle + mods[5] * result

def one_sequence(weights, image_rows, text_rows, mods_img, mods_txt, live_count):
    w_qkv_img, w_qkv_txt, w_out_img, w_out_txt, w_up_img, w_up_txt, w_down_img, w_down_txt = weights
    packed_img = project_in(image_rows, mods_img, w_qkv_img)
    packed_txt = project_in(text_rows, mods_txt, w_qkv_txt)
    joint = jnp.concatenate([packed_img, packed_txt], axis=0)
    length = joint.shape[0]
    split_view = joint.reshape(length, 3, HEADS, HEAD_DIM).transpose(1, 2, 0, 3)
    positions = jnp.arange(length, dtype=jnp.int32)
    key_live = positions < IMG + live_count

    def head_step(parts):
        return attend_head(parts[0], parts[1], parts[2], key_live)
    attended = lax.map(jax.checkpoint(head_step), (split_view[0], split_view[1], split_view[2]))
    attended = attended.transpose(1, 0, 2).reshape(length, D)
    out_img = project_out(image_rows, attended[:IMG], mods_img, w_out_img, w_up_img, w_down_img)
    out_txt = project_out(text_rows, attended[IMG:], mods_txt, w_out_txt, w_up_txt, w_down_txt)
    return (out_img, out_txt)

def forward(image_tokens, text_tokens, conditioning, w_mod_img, w_mod_txt, w_qkv_img, w_qkv_txt, w_out_img, w_out_txt, w_up_img, w_up_txt, w_down_img, w_down_txt, live_text):
    silu_cond = low(jax.nn.silu(conditioning))
    mods_img = low_back(matmul(silu_cond, w_mod_img)).reshape(-1, 6, D)
    mods_txt = low_back(matmul(silu_cond, w_mod_txt)).reshape(-1, 6, D)
    weights = (w_qkv_img, w_qkv_txt, w_out_img, w_out_txt, w_up_img, w_up_txt, w_down_img, w_down_txt)
    sequence_step = functools.partial(one_sequence, weights)

    def scan_step(carry, items):
        return (carry, sequence_step(items[0], items[1], items[2], items[3], items[4]))
    unused, outputs = lax.scan(scan_step, None, (image_tokens, text_tokens, mods_img, mods_txt, live_text))
    return outputs

def reference(image_tokens, text_tokens, conditioning, live_text, w_mod_img, w_mod_txt, w_qkv_img, w_qkv_txt, w_out_img, w_out_txt, w_up_img, w_up_txt, w_down_img, w_down_txt, image_cotangent, text_cotangent):
    floats = [item.astype(jnp.float32) for item in (image_tokens, text_tokens, conditioning, w_mod_img, w_mod_txt, w_qkv_img, w_qkv_txt, w_out_img, w_out_txt, w_up_img, w_up_txt, w_down_img, w_down_txt)]

    def run(*inputs):
        return forward(*inputs, live_text)
    outputs, pullback = jax.vjp(run, *floats)
    grads = pullback((image_cotangent.astype(jnp.float32), text_cotangent.astype(jnp.float32)))
    return (outputs[0].astype(jnp.bfloat16), outputs[1].astype(jnp.bfloat16), grads[0], grads[1], grads[2], grads[3], grads[4], grads[5], grads[6], grads[7], grads[8], grads[9], grads[10], grads[11], grads[12])
```

```python
import functools
import jax
import jax.numpy as jnp
from jax import lax
from jax.experimental import pallas as pl
from jax.experimental.pallas import tpu as pltpu
from jax.sharding import PartitionSpec as P

D = 1536
HEADS = 24
HEAD_DIM = 64
FF = 6144

epsilon = 1e-06
masked_score = -1e30
PAIR = 2 * HEAD_DIM
SCALE = HEAD_DIM ** (-0.5)
low_type = jnp.bfloat16
wide = jnp.float32


def layer_norm(values):
    centre = values - jnp.mean(values, axis=-1, keepdims=True)
    spread = jnp.mean(centre * centre, axis=-1, keepdims=True)
    return centre * lax.rsqrt(spread + epsilon)


def gelu_tanh(values):
    return jax.nn.gelu(values, approximate=True)


def dot(left, right, contract=(1, 0), out=wide):
    return lax.dot_general(
        left,
        right,
        (((contract[0],), (contract[1],)), ((), ())),
        preferred_element_type=wide,
    ).astype(out)


def head_masks():
    lane = lax.broadcasted_iota(jnp.int32, (1, PAIR), 1)
    return (lane < HEAD_DIM, lane >= HEAD_DIM)


def forward_kernel(rows, packed_ref, live_ref, out_ref):
    start = pl.multiple_of(pl.program_id(1) * rows, 16)
    query = packed_ref[pl.ds(start, rows), 0:PAIR]
    key = packed_ref[:, PAIR : 2 * PAIR]
    value = packed_ref[:, 2 * PAIR : 3 * PAIR]
    live = live_ref[...] > 0.0
    masks = head_masks()
    outs = []
    for mask in masks:
        picked = jnp.where(mask, query, 0.0) * jnp.bfloat16(SCALE)
        scores = dot(picked.astype(low_type), key, (1, 1))
        scores = jnp.where(live, scores, masked_score)
        peak = jnp.max(scores, axis=1, keepdims=True)
        weights = jnp.exp(scores - peak)
        total = jnp.sum(weights, axis=1, keepdims=True)
        probs = (weights * (1.0 / total)).astype(low_type)
        outs.append(dot(probs, value))
    out_ref[...] = jnp.where(masks[0], outs[0], outs[1]).astype(low_type)


def backward_kernel(rows, packed_ref, live_ref, grad_ref, out_ref, key_sum, value_sum):
    step = pl.program_id(1)

    @pl.when(step == 0)
    def _():
        key_sum[...] = jnp.zeros_like(key_sum)
        value_sum[...] = jnp.zeros_like(value_sum)

    start = pl.multiple_of(step * rows, 16)
    query = packed_ref[pl.ds(start, rows), 0:PAIR]
    key = packed_ref[:, PAIR : 2 * PAIR]
    value = packed_ref[:, 2 * PAIR : 3 * PAIR]
    grad = grad_ref[...]
    live = live_ref[...] > 0.0
    zero = jnp.zeros((), low_type)
    grad_query = None
    for mask in head_masks():
        key_part = jnp.where(mask, key, zero)
        key_scaled = key_part * jnp.bfloat16(SCALE)
        query_part = jnp.where(mask, query, zero)
        grad_part = jnp.where(mask, grad, zero)
        scores = dot(key_scaled, query, (1, 1))
        scores = jnp.where(live, scores, masked_score)
        peak = jnp.max(scores, axis=0, keepdims=True)
        weights = jnp.exp(scores - peak)
        total = jnp.sum(weights, axis=0, keepdims=True)
        probs = weights * (1.0 / total)
        grad_probs = dot(value, grad_part, (1, 1))
        inner = jnp.sum(probs * grad_probs, axis=0, keepdims=True)
        grad_raw = (SCALE * (probs * (grad_probs - inner))).astype(low_type)
        value_sum[...] += dot(probs.astype(low_type), grad_part)
        key_sum[...] += dot(grad_raw, query_part)
        part = dot(grad_raw, key_part, (0, 0))
        grad_query = part if grad_query is None else grad_query + part
    out_ref[pl.ds(start, rows), 0:PAIR] = grad_query.astype(low_type)

    @pl.when(step == pl.num_programs(1) - 1)
    def _():
        out_ref[:, PAIR : 2 * PAIR] = key_sum[...].astype(low_type)
        out_ref[:, 2 * PAIR : 3 * PAIR] = value_sum[...].astype(low_type)


def attention_forward(packed, live_row):
    tokens, width = packed.shape
    pairs = width // (3 * PAIR)
    steps = 2
    rows = tokens // steps
    return pl.pallas_call(
        functools.partial(forward_kernel, rows),
        grid=(pairs, steps),
        in_specs=[
            pl.BlockSpec((tokens, 3 * PAIR), lambda p, j: (0, p)),
            pl.BlockSpec((1, tokens), lambda p, j: (0, 0)),
        ],
        out_specs=pl.BlockSpec((rows, PAIR), lambda p, j: (j, p)),
        out_shape=jax.ShapeDtypeStruct((tokens, pairs * PAIR), low_type),
        compiler_params=pltpu.CompilerParams(dimension_semantics=("arbitrary", "arbitrary")),
        cost_estimate=pl.CostEstimate(
            flops=4 * tokens * tokens * pairs * PAIR,
            transcendentals=2 * pairs * tokens * tokens,
            bytes_accessed=tokens * (width + pairs * PAIR) * 2,
        ),
        name="attention_forward",
    )(packed, live_row)


def attention_backward(packed, live_column, grad):
    tokens, width = packed.shape
    pairs = width // (3 * PAIR)
    steps = 2
    rows = tokens // steps
    return pl.pallas_call(
        functools.partial(backward_kernel, rows),
        grid=(pairs, steps),
        in_specs=[
            pl.BlockSpec((tokens, 3 * PAIR), lambda p, j: (0, p)),
            pl.BlockSpec((tokens, 1), lambda p, j: (0, 0)),
            pl.BlockSpec((rows, PAIR), lambda p, j: (j, p)),
        ],
        out_specs=pl.BlockSpec((tokens, 3 * PAIR), lambda p, j: (0, p)),
        out_shape=jax.ShapeDtypeStruct((tokens, width), low_type),
        scratch_shapes=[pltpu.VMEM((tokens, PAIR), wide), pltpu.VMEM((tokens, PAIR), wide)],
        compiler_params=pltpu.CompilerParams(dimension_semantics=("arbitrary", "arbitrary")),
        cost_estimate=pl.CostEstimate(
            flops=10 * tokens * tokens * pairs * PAIR,
            transcendentals=2 * pairs * tokens * tokens,
            bytes_accessed=tokens * (2 * width + pairs * PAIR) * 2,
        ),
        name="attention_backward",
    )(packed, live_column, grad)


def on_device(
    nd,
    ns,
    image_tokens,
    text_tokens,
    conditioning,
    live_text,
    w_mod_img,
    w_mod_txt,
    w_qkv_img,
    w_qkv_txt,
    w_out_img,
    w_out_txt,
    w_up_img,
    w_up_txt,
    w_down_img,
    w_down_txt,
    image_cotangent,
    text_cotangent,
):
    assert image_tokens.shape[0] == 1
    img = image_tokens.shape[1]
    txt = text_tokens.shape[1]
    own = img + txt
    place = lax.axis_index("seq")
    head_columns = D // ns
    pairs = head_columns // PAIR
    shard = D // (nd * ns)
    hidden_block = FF // (nd * ns)
    hidden_own = FF // ns
    mod_block = 6 * D // (nd * ns)
    both = ("dp", "seq")

    def slot(k):
        return lax.rem(place + k, ns)

    def shift(values, k):
        return lax.ppermute(values, "seq", [(i, (i + k) % ns) for i in range(ns)])

    def ring_gather(values):
        held = [values]
        for _ in range(1, ns):
            held.append(shift(held[-1], -1))
        return held

    def ring_sum(parts):
        total = parts[1].astype(wide)
        for k in list(range(2, ns)) + [0]:
            total = shift(total.astype(low_type), -1).astype(wide) + parts[k].astype(wide)
        return total

    def exchange(piece):
        return [piece(k) if k == 0 else shift(piece(k), k) for k in range(ns)]

    def sources(arrived):
        return [(lax.rem(place - k + ns, ns), part) for k, part in enumerate(arrived)]

    def stack_img(chunks):
        return jnp.concatenate([c[:img] for c in chunks], axis=0)

    def stack_txt(chunks):
        return jnp.concatenate([c[img:] for c in chunks], axis=0)

    def chunk_of(images, texts, k):
        return jnp.concatenate(
            [images[k * img : (k + 1) * img], texts[k * txt : (k + 1) * txt]], axis=0
        )

    def gather_dp(values):
        return lax.all_gather(values, "dp", axis=0, tiled=True)

    def columns_to_place(pieces):
        arrived = exchange(lambda k: lax.dynamic_index_in_dim(pieces, slot(k), 0, keepdims=False))
        rows = jnp.zeros((ns,) + arrived[0].shape, low_type)
        for source, part in sources(arrived):
            rows = lax.dynamic_update_slice(rows, part[None], (source, 0, 0))
        return rows.reshape(ns * shard, -1)

    def qkv_pieces(weight):
        return (
            weight.reshape(shard, 3, ns, pairs, PAIR)
            .transpose(2, 0, 3, 1, 4)
            .reshape(ns, shard, 3 * head_columns)
        )

    def up_pieces(weight):
        return (
            weight.reshape(shard, nd, ns, hidden_block)
            .transpose(2, 0, 1, 3)
            .reshape(ns, shard, hidden_own)
        )

    tokens_own = jnp.concatenate([image_tokens[0], text_tokens[0]], axis=0)
    cotangent_own = jnp.concatenate([image_cotangent[0], text_cotangent[0]], axis=0)

    cond_all = lax.all_gather(conditioning, "dp", axis=0, tiled=True)
    silu_low = jax.nn.silu(cond_all.astype(wide)).astype(low_type)
    mod_part = jnp.stack([dot(silu_low, w_mod_img), dot(silu_low, w_mod_txt)], axis=1)
    mod_sent = jnp.broadcast_to(mod_part[:, None], (nd, ns, 2, mod_block)).reshape(
        nd * ns, 2 * mod_block
    )
    mod_here = lax.all_to_all(mod_sent, both, 0, 0, tiled=True).reshape(nd * ns, 2, mod_block)
    mods = mod_here.transpose(1, 0, 2).reshape(2, 6, D)
    mods_img, mods_txt = mods[0], mods[1]

    token_chunks = ring_gather(tokens_own)

    qkv_own = columns_to_place(
        jnp.concatenate([qkv_pieces(w_qkv_img), qkv_pieces(w_qkv_txt)], axis=2)
    )
    wq_img = gather_dp(qkv_own[:, : 3 * head_columns])
    wq_txt = gather_dp(qkv_own[:, 3 * head_columns :])
    wo_img = lax.all_gather(w_out_img, both, axis=0, tiled=True)
    wo_txt = lax.all_gather(w_out_txt, both, axis=0, tiled=True)
    up_own = columns_to_place(jnp.concatenate([up_pieces(w_up_img), up_pieces(w_up_txt)], axis=2))
    wu_img = gather_dp(up_own[:, :hidden_own])
    wu_txt = gather_dp(up_own[:, hidden_own:])
    wd_img = gather_dp(w_down_img)
    wd_txt = gather_dp(w_down_txt)

    def front(tokens, mods_kind, weight):
        normed = layer_norm(tokens.astype(wide))
        mixed = (normed * (1.0 + mods_kind[1]) + mods_kind[0]).astype(low_type)
        return (mixed, dot(mixed, weight, out=low_type))

    mixed_img, packed_img = front(stack_img(token_chunks), mods_img, wq_img)
    mixed_txt, packed_txt = front(stack_txt(token_chunks), mods_txt, wq_txt)
    packed = jnp.concatenate([packed_img, packed_txt], axis=0)
    text_index = jnp.concatenate(
        [slot(k) * txt + jnp.arange(txt, dtype=jnp.int32) for k in range(ns)]
    )
    live = jnp.concatenate(
        [jnp.ones((ns * img,), wide), (text_index < live_text[0]).astype(wide)]
    )
    attended_heads = attention_forward(packed, live[None, :])

    def piece_out(k):
        return chunk_of(attended_heads[: ns * img], attended_heads[ns * img :], k)

    attended = jnp.zeros((own, D), low_type)
    for source, part in sources(exchange(piece_out)):
        attended = lax.dynamic_update_slice(attended, part, (0, source * head_columns))

    values = tokens_own.astype(wide)

    def by_kind(row):
        return jnp.concatenate(
            [
                jnp.broadcast_to(mods_img[row], (img, D)),
                jnp.broadcast_to(mods_txt[row], (txt, D)),
            ],
            axis=0,
        )

    branch = jnp.concatenate([dot(attended[:img], wo_img), dot(attended[img:], wo_txt)], axis=0)
    middle = values + by_kind(2) * branch
    normed_late = layer_norm(middle)
    mixed_late = (normed_late * (1.0 + by_kind(4)) + by_kind(3)).astype(low_type)

    late_chunks = ring_gather(mixed_late)
    cotangent_chunks = ring_gather(cotangent_own)

    def feed(mixed, cotangent, gate, w_up, w_down):
        hidden = dot(mixed, w_up)
        activated = gelu_tanh(hidden).astype(low_type)
        result = dot(activated, w_down, out=low_type)
        grad_result = (cotangent.astype(wide) * gate).astype(low_type)
        grad_active = dot(grad_result, w_down, (1, 1))
        grad_hidden = jax.vjp(gelu_tanh, hidden)[1](grad_active)[0].astype(low_type)
        grad_mixed = dot(grad_hidden, w_up, (1, 1), low_type)
        term_down = dot(activated, grad_result, (0, 0), low_type)
        term_up = dot(mixed, grad_hidden, (0, 0), low_type)
        return (result, grad_mixed, term_up, term_down)

    result_img, late_grad_img, term_up_img, term_down_img = feed(
        stack_img(late_chunks), stack_img(cotangent_chunks), mods_img[5], wu_img, wd_img
    )
    result_txt, late_grad_txt, term_up_txt, term_down_txt = feed(
        stack_txt(late_chunks), stack_txt(cotangent_chunks), mods_txt[5], wu_txt, wd_txt
    )
    grad_mixed_late = ring_sum([chunk_of(late_grad_img, late_grad_txt, k) for k in range(ns)])
    result = ring_sum([chunk_of(result_img, result_txt, k) for k in range(ns)])

    def scatter_dp(values):
        return lax.psum_scatter(values, "dp", scatter_dimension=0, tiled=True)

    grad_down_img = scatter_dp(term_down_img).astype(wide)
    grad_down_txt = scatter_dp(term_down_txt).astype(wide)

    def rows_to_owner(terms):
        pieces = terms.reshape(ns, shard, -1)
        return sources(
            exchange(lambda k: lax.dynamic_index_in_dim(pieces, slot(k), 0, keepdims=False))
        )

    up_terms = rows_to_owner(
        jnp.concatenate([scatter_dp(term_up_img), scatter_dp(term_up_txt)], axis=1)
    )

    def place_up(start):
        out = jnp.zeros((shard, nd, ns, hidden_block), wide)
        for source, part in up_terms:
            part = part[:, start : start + hidden_own].astype(wide)
            out = lax.dynamic_update_slice(
                out, part.reshape(shard, nd, 1, hidden_block), (0, 0, source, 0)
            )
        return out.reshape(shard, FF)

    grad_up_img, grad_up_txt = place_up(0), place_up(hidden_own)

    output = (middle + by_kind(5) * result).astype(low_type)
    grad_output = cotangent_own.astype(wide)
    grad_middle = grad_output + jax.vjp(layer_norm, middle)[1](
        grad_mixed_late * (1.0 + by_kind(4))
    )[0]
    grad_branch = (grad_middle * by_kind(2)).astype(low_type)
    grad_attended = jnp.concatenate(
        [
            dot(grad_branch[:img], wo_img, (1, 1), low_type),
            dot(grad_branch[img:], wo_txt, (1, 1), low_type),
        ],
        axis=0,
    )
    arrived = exchange(
        lambda k: lax.dynamic_slice_in_dim(
            grad_attended, slot(k) * head_columns, head_columns, axis=1
        )
    )
    grad_chunks = [arrived[-k % ns] for k in range(ns)]
    grad_heads = jnp.concatenate([stack_img(grad_chunks), stack_txt(grad_chunks)], axis=0)
    term_out_img = dot(attended[:img], grad_branch[:img], (0, 0), low_type)
    term_out_txt = dot(attended[img:], grad_branch[img:], (0, 0), low_type)

    grad_packed = attention_backward(packed, live[:, None], grad_heads)
    packed_grad_img, packed_grad_txt = grad_packed[: ns * img], grad_packed[ns * img :]
    early_grad_img = dot(packed_grad_img, wq_img, (1, 1), low_type)
    early_grad_txt = dot(packed_grad_txt, wq_txt, (1, 1), low_type)
    grad_mixed = ring_sum([chunk_of(early_grad_img, early_grad_txt, k) for k in range(ns)])
    term_qkv_img = dot(mixed_img, packed_grad_img, (0, 0), low_type)
    term_qkv_txt = dot(mixed_txt, packed_grad_txt, (0, 0), low_type)

    def scatter_all(values):
        return lax.psum_scatter(values, both, scatter_dimension=0, tiled=True).astype(wide)

    grad_out_img, grad_out_txt = scatter_all(term_out_img), scatter_all(term_out_txt)
    qkv_terms = rows_to_owner(
        jnp.concatenate([scatter_dp(term_qkv_img), scatter_dp(term_qkv_txt)], axis=1)
    )

    def place_qkv(start):
        out = jnp.zeros((shard, 3, ns, pairs, PAIR), wide)
        for source, part in qkv_terms:
            part = part[:, start : start + 3 * head_columns].astype(wide)
            part = part.reshape(shard, pairs, 3, PAIR).transpose(0, 2, 1, 3)
            out = lax.dynamic_update_slice(out, part[:, :, None], (0, 0, source, 0, 0))
        return out.reshape(shard, 3 * D)

    grad_qkv_img, grad_qkv_txt = place_qkv(0), place_qkv(3 * head_columns)

    normed = layer_norm(values)
    grad_input = grad_middle + jax.vjp(layer_norm, values)[1](
        grad_mixed * (1.0 + by_kind(1))
    )[0]

    def sums(terms):
        return jnp.stack([jnp.sum(terms[:img], axis=0), jnp.sum(terms[img:], axis=0)])

    grad_mods = jnp.stack(
        [
            sums(grad_mixed),
            sums(grad_mixed * normed),
            sums(grad_middle * branch),
            sums(grad_mixed_late),
            sums(grad_mixed_late * normed_late),
            sums(grad_output * result),
        ],
        axis=1,
    )
    mods_sent = (
        grad_mods.reshape(2, nd * ns, mod_block)
        .transpose(1, 0, 2)
        .reshape(nd * ns, 2 * mod_block)
    )
    mods_back = lax.all_to_all(mods_sent, both, 0, 0, tiled=True)
    modulation = jnp.sum(mods_back.reshape(nd, ns, 2, mod_block), axis=1).astype(low_type)
    modulation_img, modulation_txt = modulation[:, 0], modulation[:, 1]
    grad_mod_img = dot(silu_low, modulation_img, (0, 0))
    grad_mod_txt = dot(silu_low, modulation_txt, (0, 0))
    silu_grad = dot(modulation_img, w_mod_img, (1, 1)) + dot(modulation_txt, w_mod_txt, (1, 1))
    cond_sent = jnp.broadcast_to(silu_grad[:, None], (nd, ns, D)).reshape(nd * ns, D)
    cond_back = lax.all_to_all(cond_sent, both, 0, 0, tiled=True)
    cond_total = jnp.sum(cond_back, axis=0, keepdims=True)
    grad_cond = jax.vjp(jax.nn.silu, conditioning.astype(wide))[1](cond_total)[0]

    return (
        output[None, :img],
        output[None, img:],
        grad_input[None, :img],
        grad_input[None, img:],
        grad_cond,
        grad_mod_img,
        grad_mod_txt,
        grad_qkv_img,
        grad_qkv_txt,
        grad_out_img,
        grad_out_txt,
        grad_up_img,
        grad_up_txt,
        grad_down_img,
        grad_down_txt,
    )


def solution(mesh):
    token = P("dp", "seq", None)
    columns = P(None, ("dp", "seq"))
    rows = P(("dp", "seq"), None)
    in_specs = (
        (token, token, P("dp", None), P("dp"), columns, columns) + (rows,) * 8 + (token, token)
    )
    out_specs = (token,) * 4 + (P("dp", None), columns, columns) + (rows,) * 8
    return jax.shard_map(
        functools.partial(on_device, mesh.shape["dp"], mesh.shape["seq"]),
        mesh=mesh,
        in_specs=in_specs,
        out_specs=out_specs,
        check_vma=False,
    )
```
